32 devices in a mesh: dp: 4 (over x, core), shard: 8 (over z, y).
Axes of the slice: x: 2, y: 2, z: 4, core: 2. Of those that a mesh axis runs over, the one named last changes fastest.
Arguments:
- tokens: bfloat16 [256, 6144], P('dp', 'shard'), may hold values from -6 to 6
- cotangent: bfloat16 [256, 6144], P('dp', 'shard'), may hold values from -12 to 12
- gate_proj: bfloat16 [2, 6144, 16384], P(None, 'dp', 'shard'), may hold values from -0.078125 to 0.078125
- up_proj: bfloat16 [2, 6144, 16384], P(None, 'dp', 'shard'), may hold values from -0.078125 to 0.078125
- down_proj: bfloat16 [2, 16384, 6144], P(None, 'shard', 'dp'), may hold values from -0.046875 to 0.046875
- slot_tokens: int32 [2, 64], P(None, 'dp'), may hold values from 0 to 63, as said below
- gate_weights: float32 [2, 64], P(None, 'dp'), may hold values from 0.1 to 1
- live_counts: int32 [2, 4], P(None, 'dp'), may hold values from 1 to 16, as said below
Outputs:
- grad_tokens: bfloat16 [256, 6144], P('dp', 'shard')
- grad_gate_proj: bfloat16 [2, 6144, 16384], P(None, 'dp', 'shard')
- grad_up_proj: bfloat16 [2, 6144, 16384], P(None, 'dp', 'shard')
- grad_down_proj: bfloat16 [2, 16384, 6144], P(None, 'shard', 'dp')
The draws below stay inside these ranges and needn't reach their ends.
Inputs may be any that keep to these rules, and one draw needn't show every extreme that they name: `slot_tokens`: for each expert and each index of dp, the 16 slots name 16 different tokens of that index. `live_counts`: the live slots of an expert at an index of dp are its first ones; 16 is reached at some index of every expert.
All inputs are finite; a program needn't handle non-finite values.
Results may differ from the reference program's by a relative error of at most 0.03.
Values may be sent and summed in bfloat16 or wider, within the bound.
A program may use at most 128 MiB of HBM per device.

```python
import jax
import jax.numpy as jnp
from jax import lax

D = 6144
FF = 16384
EXPERTS = 2
ROWS = 16
TOK_DEV = 64
TOKENS = 256
ROUTED = 64
N_DP = 4
N_SHARD = 8


def draw_slot_tokens(key, part):
    shape = (EXPERTS, N_DP, TOK_DEV)
    scores = jax.random.randint(key, shape, 0, 1 << 20)
    scores = scores * TOK_DEV + lax.broadcasted_iota(jnp.int32, shape, 2)
    chosen = jnp.argsort(scores, axis=2, stable=True)[:, :, :ROWS]
    return chosen.reshape(EXPERTS, N_DP * ROWS).astype(jnp.int32)


def draw_live_counts(key, part):
    lowest = max(ROWS // 3, 1)
    position = lax.broadcasted_iota(jnp.int32, (EXPERTS, N_DP), 1)
    rising = lowest + position * (ROWS - lowest) // max(N_DP - 1, 1)
    jitter = jax.random.randint(key, (EXPERTS, N_DP), -2, 3)
    drawn = jnp.clip(rising + jitter, 1, ROWS)
    return jnp.where(position == N_DP - 1, ROWS, drawn).astype(jnp.int32)


def shard_levels(key, shape, shards, least, top_value):
    gain, own = 1.0, jax.random.fold_in(key, 6)
    for dim, shards_of in shards:
        heights = jnp.exp(jax.random.uniform(jax.random.fold_in(own, dim), (shards_of,), jnp.float32, least / len(shards), top_value / len(shards)))
        gain = gain * jnp.repeat(heights, shape[dim] // shards_of).reshape([-1 if axis == dim else 1 for axis in range(len(shape))])
    return gain


def centred(key, dims, spread, reach, shards=(), kind=jnp.bfloat16):
    values = jax.random.normal(key, dims, jnp.float32) * spread
    if len(shards) > 0:
        values = shard_levels(key, dims, shards, -0.22, 0.18) * values
    return jnp.clip(values, min=-reach, max=reach).astype(kind)


def setup_inputs(seed: int = 0) -> dict:
    streams_of = jax.random.split(jax.random.key(seed), 9)
    tokens = centred(streams_of[0], (TOKENS, D), 1.0, 6.0, ((0, 4), (1, 8)))
    cotangent = centred(streams_of[1], (TOKENS, D), 2.0, 12.0, ((0, 4), (1, 8)))
    gate_proj = centred(streams_of[2], (EXPERTS, D, FF), D ** -0.5, 0.078125, ((1, 4), (2, 8)))
    up_proj = centred(streams_of[3], (EXPERTS, D, FF), D ** -0.5, 0.078125, ((1, 4), (2, 8)))
    down_proj = centred(streams_of[4], (EXPERTS, FF, D), FF ** -0.5, 0.046875, ((1, 8), (2, 4)))
    slot_tokens = draw_slot_tokens(jax.random.fold_in(streams_of[8], 71), 0)
    gate_weights = jnp.clip(0.1 + 0.9 * jax.random.uniform(streams_of[6], (EXPERTS, ROUTED), jnp.float32) ** shard_levels(streams_of[6], (EXPERTS, ROUTED), ((1, 4),), -0.2, 0.2), 0.1, 1.0)
    live_counts = draw_live_counts(jax.random.fold_in(streams_of[8], 71), 0)
    return {"tokens": tokens, "cotangent": cotangent, "gate_proj": gate_proj, "up_proj": up_proj, "down_proj": down_proj, "slot_tokens": slot_tokens, "gate_weights": gate_weights, "live_counts": live_counts}


def rounded(term):
    return lax.optimization_barrier(term.astype(jnp.bfloat16)).astype(jnp.float32)


def slope_terms(gate_sum, up_sum, cot_hidden):
    sigmoid_part = jax.nn.sigmoid(gate_sum)
    grad_gate = (cot_hidden * up_sum * sigmoid_part * (1.0 + gate_sum * (1.0 - sigmoid_part))).astype(jnp.bfloat16)
    grad_up = (cot_hidden * gate_sum * sigmoid_part).astype(jnp.bfloat16)
    return grad_gate, grad_up


def reference(tokens, cotangent, gate_proj, up_proj, down_proj, slot_tokens, gate_weights, live_counts):
    routed = N_DP * ROWS
    position = lax.broadcasted_iota(jnp.int32, (EXPERTS, routed), 1)
    owner = (position // ROWS).astype(jnp.int32)
    places = (slot_tokens + owner * TOK_DEV).astype(jnp.int32)
    alive_mask = ((position % ROWS) < jnp.take_along_axis(live_counts, owner, axis=1)).astype(jnp.float32)
    picked = tokens[places]
    weighted = (cotangent[places].astype(jnp.float32) * (gate_weights * alive_mask)[:, :, None]).astype(jnp.bfloat16)
    totals = jnp.sum(live_counts, axis=1).astype(jnp.float32)
    picked_wide = picked.astype(jnp.float32)
    weighted_wide = weighted.astype(jnp.float32)
    span = D // N_DP
    blocks_dp = jnp.arange(N_DP, dtype=jnp.int32)

    def input_block(carry, block):
        start = block * span
        rows_part = lax.dynamic_slice_in_dim(picked_wide, start, span, 2)
        gate_rows = lax.dynamic_slice_in_dim(gate_proj, start, span, 1).astype(jnp.float32)
        up_rows = lax.dynamic_slice_in_dim(up_proj, start, span, 1).astype(jnp.float32)
        gate_part = jnp.einsum('erd,edf->erf', rows_part, gate_rows)
        up_part = jnp.einsum('erd,edf->erf', rows_part, up_rows)
        return (carry[0] + rounded(gate_part), carry[1] + rounded(up_part)), None

    zeros_hidden = jnp.zeros((EXPERTS, routed, FF), jnp.float32)
    (gate_sum, up_sum), _ = lax.scan(input_block, (zeros_hidden, zeros_hidden), blocks_dp)
    hidden = (jax.nn.silu(gate_sum) * up_sum).astype(jnp.bfloat16)

    def cot_block(carry, block):
        start = block * span
        cot_part = lax.dynamic_slice_in_dim(weighted_wide, start, span, 2)
        down_cols = lax.dynamic_slice_in_dim(down_proj, start, span, 2).astype(jnp.float32)
        return carry + rounded(jnp.einsum('erd,efd->erf', cot_part, down_cols)), None

    cot_hidden, _ = lax.scan(cot_block, zeros_hidden, blocks_dp)
    grad_gate, grad_up = slope_terms(gate_sum, up_sum, cot_hidden)

    def expert_grads(pieces):
        rows_in, cot_in, hidden_in, gate_in, up_in, total = pieces
        gate_grad = (jnp.dot(rows_in.T, gate_in, preferred_element_type=jnp.float32) / total).astype(jnp.bfloat16)
        up_grad = (jnp.dot(rows_in.T, up_in, preferred_element_type=jnp.float32) / total).astype(jnp.bfloat16)
        down_grad = (jnp.dot(hidden_in.T, cot_in, preferred_element_type=jnp.float32) / total).astype(jnp.bfloat16)
        return gate_grad, up_grad, down_grad

    grad_gate_proj, grad_up_proj, grad_down_proj = lax.map(
        expert_grads, (picked, weighted, hidden, grad_gate, grad_up, totals))

    width = FF // N_SHARD
    gate_wide = grad_gate.astype(jnp.float32)
    up_wide = grad_up.astype(jnp.float32)

    def back_block(carry, block):
        start = block * width
        gate_cols = lax.dynamic_slice_in_dim(gate_wide, start, width, 2)
        up_cols = lax.dynamic_slice_in_dim(up_wide, start, width, 2)
        gate_mat = lax.dynamic_slice_in_dim(gate_proj, start, width, 2).astype(jnp.float32)
        up_mat = lax.dynamic_slice_in_dim(up_proj, start, width, 2).astype(jnp.float32)
        term = jnp.einsum('erf,edf->erd', gate_cols, gate_mat) + jnp.einsum('erf,edf->erd', up_cols, up_mat)
        return carry + rounded(term), None

    grad_rows, _ = lax.scan(back_block, jnp.zeros((EXPERTS, routed, D), jnp.float32),
                            jnp.arange(N_SHARD, dtype=jnp.int32))
    grad_tokens = jnp.zeros((TOKENS, D), jnp.float32).at[places.reshape(-1)].add(
        grad_rows.reshape(EXPERTS * routed, D)).astype(jnp.bfloat16)
    return grad_tokens, grad_gate_proj, grad_up_proj, grad_down_proj
```

```python
import functools

import jax
import jax.numpy as jnp
from jax import lax
from jax.experimental import pallas as pl
from jax.experimental.pallas import tpu as pltpu
from jax.sharding import PartitionSpec as P

MESH = pl.DeviceIdType.MESH
PIECES = 2


def slope_terms(gate_sum, up_sum, cot_hidden):
    sigmoid_part = jax.nn.sigmoid(gate_sum)
    grad_gate = (
        cot_hidden * up_sum * sigmoid_part * (1.0 + gate_sum * (1.0 - sigmoid_part))
    ).astype(jnp.bfloat16)
    grad_up = (cot_hidden * gate_sum * sigmoid_part).astype(jnp.bfloat16)
    return (grad_gate, grad_up)


def on_device(
    tokens, cotangent, gate_proj, up_proj, down_proj, slot_tokens, gate_weights, live_counts
):
    experts_here = slot_tokens.shape[0]
    slot_count = slot_tokens.shape[1]
    token_count = tokens.shape[0]
    position = lax.broadcasted_iota(jnp.int32, slot_tokens.shape, 1)
    alive_mask = (position < live_counts).astype(jnp.float32)
    picked = tokens[slot_tokens]
    weighted = (
        cotangent[slot_tokens].astype(jnp.float32) * (gate_weights * alive_mask)[:, :, None]
    ).astype(jnp.bfloat16)
    full_rows, full_cot = (
        lax.all_gather(picked, "shard", axis=2, tiled=True),
        lax.all_gather(weighted, "shard", axis=2, tiled=True),
    )
    block_rows, block_cot = (
        lax.all_to_all(full_rows, "dp", split_axis=2, concat_axis=1, tiled=True),
        lax.all_to_all(full_cot, "dp", split_axis=2, concat_axis=1, tiled=True),
    )
    totals = lax.psum(live_counts, "dp").astype(jnp.float32)
    gate_part = jnp.einsum(
        "erd,edf->erf", block_rows, gate_proj, preferred_element_type=jnp.float32
    )
    up_part = jnp.einsum("erd,edf->erf", block_rows, up_proj, preferred_element_type=jnp.float32)
    cot_part = jnp.einsum("erd,efd->erf", block_cot, down_proj, preferred_element_type=jnp.float32)
    gate_total, up_total = (
        lax.psum(gate_part.astype(jnp.bfloat16), "dp").astype(jnp.float32),
        lax.psum(up_part.astype(jnp.bfloat16), "dp").astype(jnp.float32),
    )
    hidden_all = (jax.nn.silu(gate_total) * up_total).astype(jnp.bfloat16)
    cot_total = lax.psum(cot_part.astype(jnp.bfloat16), "dp").astype(jnp.float32)
    gate_all, up_all = slope_terms(gate_total, up_total, cot_total)
    scale_back = totals[:, :, None]
    grad_down_proj = (
        jnp.einsum("erf,erd->efd", hidden_all, block_cot, preferred_element_type=jnp.float32)
        / scale_back
    ).astype(jnp.bfloat16)
    grad_gate_proj = (
        jnp.einsum("erd,erf->edf", block_rows, gate_all, preferred_element_type=jnp.float32)
        / scale_back
    ).astype(jnp.bfloat16)
    grad_up_proj = (
        jnp.einsum("erd,erf->edf", block_rows, up_all, preferred_element_type=jnp.float32)
        / scale_back
    ).astype(jnp.bfloat16)
    back_term = (
        jnp.einsum("erf,edf->erd", gate_all, gate_proj, preferred_element_type=jnp.float32)
        + jnp.einsum("erf,edf->erd", up_all, up_proj, preferred_element_type=jnp.float32)
    ).astype(jnp.bfloat16)
    owned_rows = lax.all_to_all(back_term, "dp", split_axis=1, concat_axis=2, tiled=True)
    row_grads = lax.psum_scatter(
        owned_rows.astype(jnp.float32).astype(jnp.bfloat16),
        "shard",
        scatter_dimension=2,
        tiled=True,
    ).astype(jnp.float32)
    one_hot = (
        slot_tokens[:, :, None]
        == lax.broadcasted_iota(jnp.int32, (experts_here, slot_count, token_count), 2)
    ).astype(jnp.float32)
    grad_tokens = jnp.einsum("ert,erf->tf", one_hot, row_grads).astype(jnp.bfloat16)
    return (grad_tokens, grad_gate_proj, grad_up_proj, grad_down_proj)


def step_kernel(
    n_dp, n_shard,
    slot_col, slot_row, scale_col, counts, tokens, cot, gate_hbm, up_hbm, down_hbm,
    rows_out, cotr_out, hid_out, gg_out, gu_out, tot_out, tok_out,
    gate_w, up_w, down_w, pick, wcot, mine, psend, precv, xsend, xrecv, back, parts, cnt_in,
    w_sem, g_send, g_recv, p_send, p_recv, x_send, x_recv, a_send, a_recv, r_send, r_recv,
):
    d = lax.axis_index("dp")
    s = lax.axis_index("shard")
    experts, depth, width = gate_w.shape
    feats = tokens.shape[1]
    slots = slot_col.shape[0] // experts
    per = n_shard // n_dp
    core = d % 2
    pair = d + 1 - 2 * core
    across = (d + 2) % 4
    half = width // 2
    piece = half // PIECES

    loads = []
    for e in range(experts):
        for i, (src, dst) in enumerate(((gate_hbm, gate_w), (up_hbm, up_w), (down_hbm, down_w))):
            load = pltpu.make_async_copy(src.at[e], dst.at[e], w_sem.at[i, e])
            load.start()
            loads.append(load)

    barrier = pltpu.get_barrier_semaphore()
    owner = s // per
    for t in range(n_shard):
        pl.semaphore_signal(barrier, inc=1, device_id={"dp": owner, "shard": t}, device_id_type=MESH)
    for e in range(n_dp):
        for k in range(per):
            pl.semaphore_signal(
                barrier, inc=1, device_id={"dp": e, "shard": d * per + k}, device_id_type=MESH
            )
    for peer in (pair, across):
        pl.semaphore_signal(barrier, inc=1, device_id={"dp": peer, "shard": s}, device_id_type=MESH)

    token_ids = lax.broadcasted_iota(jnp.int32, (experts * slots, tokens.shape[0]), 1)
    choose = (slot_col[...] == token_ids).astype(jnp.float32).astype(jnp.bfloat16)
    pick_all = jnp.dot(choose, tokens[...], preferred_element_type=jnp.float32)
    cot_all = jnp.dot(choose, cot[...], preferred_element_type=jnp.float32)
    cot_all = (cot_all * scale_col[...]).astype(jnp.bfloat16)
    pick_all = pick_all.astype(jnp.bfloat16)
    for e in range(experts):
        pick[e] = pick_all[e * slots : (e + 1) * slots]
        wcot[e] = cot_all[e * slots : (e + 1) * slots]

    pl.semaphore_wait(barrier, n_shard + n_dp * per + 2)

    k_me = s % per
    at_me = d * per + k_me
    row_me = pl.ds(pl.multiple_of(d * slots, slots), slots)
    col_me = pl.ds(pl.multiple_of(k_me * feats, 128), feats)
    sends = []

    def send_to(target, is_self, pairs, send_sem_of, recv_sem_of):
        for i, (src, dst) in enumerate(pairs):
            remote = pltpu.make_async_remote_copy(
                src_ref=src, dst_ref=dst, send_sem=send_sem_of(i), recv_sem=recv_sem_of(i),
                device_id=target, device_id_type=MESH,
            )

            @pl.when(jnp.logical_not(is_self))
            def _():
                remote.start()

            @pl.when(is_self)
            def _():
                pltpu.make_async_copy(src, dst, recv_sem_of(i)).start()

            sends.append((remote, is_self))

    gather_pairs = (
        (pick, rows_out.at[:, row_me, col_me]),
        (wcot, cotr_out.at[:, row_me, col_me]),
        (counts, cnt_in.at[at_me]),
    )
    for step in range(n_shard):
        t = (s + step) % n_shard
        send_to(
            {"dp": owner, "shard": t},
            jnp.logical_and(owner == d, t == s),
            gather_pairs,
            lambda i: g_send.at[i, step],
            lambda i: g_recv.at[i, at_me],
        )
    for e in range(n_dp):
        for k in range(per):
            at = e * per + k
            r = pl.ds(e * slots, slots)
            c = pl.ds(k * feats, feats)
            for i, dst in enumerate(
                (rows_out.at[:, r, c], cotr_out.at[:, r, c], cnt_in.at[at])
            ):
                pltpu.make_async_copy(dst, dst, g_recv.at[i, at]).wait()
    total = cnt_in[0]
    for e in range(1, n_dp):
        total = total + cnt_in[e * per]
    tot_out[...] = total

    stages = [(e, j) for e in range(experts) for j in range(PIECES)]

    def columns(who, j):
        return pl.ds(pl.multiple_of(who * half + j * piece, 128), piece)

    def partials(e, cols):
        rows = rows_out[e]
        gate = jnp.dot(rows, gate_w[e, :, cols], preferred_element_type=jnp.float32)
        up = jnp.dot(rows, up_w[e, :, cols], preferred_element_type=jnp.float32)
        down = lax.dot_general(
            cotr_out[e], down_w[e, cols, :], (((1,), (1,)), ((), ())),
            preferred_element_type=jnp.float32,
        )
        return gate, up, down

    def pair_copy(t):
        return pltpu.make_async_remote_copy(
            src_ref=psend.at[t], dst_ref=precv.at[t], send_sem=p_send.at[t], recv_sem=p_recv.at[t],
            device_id={"dp": pair, "shard": s}, device_id_type=MESH,
        )

    def across_copy(t):
        return pltpu.make_async_remote_copy(
            src_ref=xsend.at[t], dst_ref=xrecv.at[t], send_sem=x_send.at[t], recv_sem=x_recv.at[t],
            device_id={"dp": across, "shard": s}, device_id_type=MESH,
        )

    def back_copies(t, who):
        e, j = stages[t]
        cols = columns(who, j)
        return [
            pltpu.make_async_remote_copy(
                src_ref=out.at[e, :, cols], dst_ref=out.at[e, :, cols],
                send_sem=a_send.at[i, t], recv_sem=a_recv.at[i, t],
                device_id={"dp": pair, "shard": s}, device_id_type=MESH,
            )
            for i, out in enumerate((hid_out, gg_out, gu_out))
        ]

    def compute(t):
        e, j = stages[t]
        if j == 0:
            for load in loads[3 * e : 3 * e + 3]:
                load.wait()
        for i, value in enumerate(partials(e, columns(1 - core, j))):
            psend[t, i] = value.astype(jnp.bfloat16)
        pair_copy(t).start()
        for i, value in enumerate(partials(e, columns(core, j))):
            mine[t, i] = value.astype(jnp.bfloat16)

    def add_pair(t):
        pair_copy(t).wait_recv()
        both = mine[t].astype(jnp.float32) + precv[t].astype(jnp.float32)
        xsend[t] = both.astype(jnp.bfloat16)
        across_copy(t).start()

    def finish(t):
        e, j = stages[t]
        across_copy(t).wait_recv()
        gate = xsend[t, 0].astype(jnp.float32) + xrecv[t, 0].astype(jnp.float32)
        up = xsend[t, 1].astype(jnp.float32) + xrecv[t, 1].astype(jnp.float32)
        cot_hidden = xsend[t, 2].astype(jnp.float32) + xrecv[t, 2].astype(jnp.float32)
        cols = columns(core, j)
        hid_out[e, :, cols] = (jax.nn.silu(gate) * up).astype(jnp.bfloat16)
        grad_gate, grad_up = slope_terms(gate, up, cot_hidden)
        gg_out[e, :, cols] = grad_gate
        gu_out[e, :, cols] = grad_up
        for copy in back_copies(t, core):
            copy.start()

    def backward(e):
        for t, (te, _) in enumerate(stages):
            if te == e:
                for copy in back_copies(t, 1 - core):
                    copy.wait_recv()
        contract = (((1,), (1,)), ((), ()))
        block = 256 if depth % 256 == 0 else depth
        for b in range(depth // block):
            r = pl.ds(b * block, block)
            term = lax.dot_general(
                gg_out[e], gate_w[e, r, :], contract, preferred_element_type=jnp.float32
            ) + lax.dot_general(
                gu_out[e], up_w[e, r, :], contract, preferred_element_type=jnp.float32
            )
            back[e, :, r] = term.astype(jnp.bfloat16)
        for step in range(n_dp):
            who = (d + step) % n_dp
            r = pl.ds(pl.multiple_of(who * slots, slots), slots)
            for k in range(per):
                send_to(
                    {"dp": who, "shard": d * per + k},
                    jnp.logical_and(who == d, d * per + k == s),
                    ((back.at[e, r, pl.ds(k * feats, feats)], parts.at[e, s]),),
                    lambda i: r_send.at[e, step * per + k],
                    lambda i: r_recv.at[e, s],
                )

    last = len(stages)
    for t in range(last):
        compute(t)
        if t >= 1:
            add_pair(t - 1)
        if t >= 2:
            finish(t - 2)
    add_pair(last - 1)
    finish(last - 2)
    for e in range(experts - 1):
        backward(e)
    finish(last - 1)
    backward(experts - 1)

    choose_back = (
        slot_row[...] == lax.broadcasted_iota(jnp.int32, (tokens.shape[0], experts * slots), 0)
    ).astype(jnp.float32)
    sums = []
    for e in range(experts):
        for t in range(n_shard):
            pltpu.make_async_copy(parts.at[e, t], parts.at[e, t], r_recv.at[e, t]).wait()
        acc = parts[e, 0].astype(jnp.float32)
        for t in range(1, n_shard):
            acc = acc + parts[e, t].astype(jnp.float32)
        sums.append(acc)
    tok_out[...] = jnp.dot(
        choose_back, jnp.concatenate(sums, axis=0),
        preferred_element_type=jnp.float32, precision=lax.Precision.HIGHEST,
    ).astype(jnp.bfloat16)

    for t in range(last):
        pair_copy(t).wait_send()
        across_copy(t).wait_send()
        for copy in back_copies(t, core):
            copy.wait_send()
    for remote, is_self in sends:

        @pl.when(jnp.logical_not(is_self))
        def _():
            remote.wait_send()


def on_device_fused(
    n_dp, n_shard,
    tokens, cotangent, gate_proj, up_proj, down_proj, slot_tokens, gate_weights, live_counts,
):
    experts, slots = slot_tokens.shape
    depth, width = gate_proj.shape[1:]
    feats = tokens.shape[1]
    routed = slots * n_dp
    per = n_shard // n_dp
    position = lax.broadcasted_iota(jnp.int32, slot_tokens.shape, 1)
    alive_mask = (position < live_counts).astype(jnp.float32)
    scale_col = (gate_weights * alive_mask).reshape(-1, 1)
    counts = jnp.broadcast_to(
        jnp.pad(live_counts, ((0, 8 - experts), (0, 0))), (8, 128)
    ).astype(jnp.int32)
    stages = experts * PIECES
    piece = width // 2 // PIECES
    vmem = pl.BlockSpec(memory_space=pltpu.VMEM)
    hbm = pl.BlockSpec(memory_space=pl.ANY)
    bf16 = jnp.bfloat16
    dma = pltpu.SemaphoreType.DMA
    block = pltpu.VMEM((stages, 3, routed, piece), bf16)
    outs = pl.pallas_call(
        functools.partial(step_kernel, n_dp, n_shard),
        out_shape=(
            jax.ShapeDtypeStruct((experts, routed, depth), bf16),
            jax.ShapeDtypeStruct((experts, routed, depth), bf16),
            jax.ShapeDtypeStruct((experts, routed, width), bf16),
            jax.ShapeDtypeStruct((experts, routed, width), bf16),
            jax.ShapeDtypeStruct((experts, routed, width), bf16),
            jax.ShapeDtypeStruct((8, 128), jnp.int32),
            jax.ShapeDtypeStruct(tokens.shape, bf16),
        ),
        in_specs=[vmem] * 6 + [hbm] * 3,
        out_specs=(vmem,) * 7,
        scratch_shapes=[
            pltpu.VMEM((experts, depth, width), bf16),
            pltpu.VMEM((experts, depth, width), bf16),
            pltpu.VMEM((experts, width, depth), bf16),
            pltpu.VMEM((experts, slots, feats), bf16),
            pltpu.VMEM((experts, slots, feats), bf16),
            block, block, block, block, block,
            pltpu.VMEM((experts, routed, depth), bf16),
            pltpu.VMEM((experts, n_shard, slots, feats), bf16),
            pltpu.VMEM((n_dp * per, 8, 128), jnp.int32),
            dma((3, experts)),
            dma((3, n_shard)), dma((3, n_dp * per)),
            dma((stages,)), dma((stages,)), dma((stages,)), dma((stages,)),
            dma((3, stages)), dma((3, stages)),
            dma((experts, n_dp * per)), dma((experts, n_shard)),
        ],
        compiler_params=pltpu.CompilerParams(
            collective_id=0, has_side_effects=True, vmem_limit_bytes=62 * 1024 * 1024
        ),
        name="route_step",
    )(
        slot_tokens.reshape(-1, 1), slot_tokens.reshape(1, -1), scale_col, counts,
        tokens, cotangent, gate_proj, up_proj, down_proj,
    )
    block_rows, block_cot, hidden_all, gate_all, up_all, totals, grad_tokens = outs
    scale_back = totals[:experts, :1].astype(jnp.float32)[:, :, None]
    grad_down_proj = (
        jnp.einsum("erf,erd->efd", hidden_all, block_cot, preferred_element_type=jnp.float32)
        / scale_back
    ).astype(jnp.bfloat16)
    grad_gate_proj = (
        jnp.einsum("erd,erf->edf", block_rows, gate_all, preferred_element_type=jnp.float32)
        / scale_back
    ).astype(jnp.bfloat16)
    grad_up_proj = (
        jnp.einsum("erd,erf->edf", block_rows, up_all, preferred_element_type=jnp.float32)
        / scale_back
    ).astype(jnp.bfloat16)
    return (grad_tokens, grad_gate_proj, grad_up_proj, grad_down_proj)


def pick_form(n_dp, n_shard, *args):
    feats = args[0].shape[1]
    aligned = feats % 128 == 0 and args[2].shape[2] % (256 * PIECES) == 0
    if n_dp == 4 and n_shard % n_dp == 0 and aligned and args[5].shape[1] % 16 == 0:
        return on_device_fused(n_dp, n_shard, *args)
    return on_device(*args)


def solution(mesh):
    in_specs = (
        P("dp", "shard"),
        P("dp", "shard"),
        P(None, "dp", "shard"),
        P(None, "dp", "shard"),
        P(None, "shard", "dp"),
        P(None, "dp"),
        P(None, "dp"),
        P(None, "dp"),
    )
    out_specs = (
        P("dp", "shard"),
        P(None, "dp", "shard"),
        P(None, "dp", "shard"),
        P(None, "shard", "dp"),
    )
    return jax.shard_map(
        functools.partial(pick_form, mesh.shape["dp"], mesh.shape["shard"]), mesh=mesh, in_specs=in_specs, out_specs=out_specs, check_vma=False
    )
```

```python
import functools

import jax
import jax.numpy as jnp
from jax import lax
from jax.experimental import pallas as pl
from jax.experimental.pallas import tpu as pltpu
from jax.sharding import PartitionSpec as P

MESH = pl.DeviceIdType.MESH
PIECES = 2


def slope_terms(gate_sum, up_sum, cot_hidden):
    sigmoid_part = jax.nn.sigmoid(gate_sum)
    grad_gate = (
        cot_hidden * up_sum * sigmoid_part * (1.0 + gate_sum * (1.0 - sigmoid_part))
    ).astype(jnp.bfloat16)
    grad_up = (cot_hidden * gate_sum * sigmoid_part).astype(jnp.bfloat16)
    return (grad_gate, grad_up)


def on_device(
    tokens, cotangent, gate_proj, up_proj, down_proj, slot_tokens, gate_weights, live_counts
):
    experts_here = slot_tokens.shape[0]
    slot_count = slot_tokens.shape[1]
    token_count = tokens.shape[0]
    position = lax.broadcasted_iota(jnp.int32, slot_tokens.shape, 1)
    alive_mask = (position < live_counts).astype(jnp.float32)
    picked = tokens[slot_tokens]
    weighted = (
        cotangent[slot_tokens].astype(jnp.float32) * (gate_weights * alive_mask)[:, :, None]
    ).astype(jnp.bfloat16)
    full_rows, full_cot = (
        lax.all_gather(picked, "shard", axis=2, tiled=True),
        lax.all_gather(weighted, "shard", axis=2, tiled=True),
    )
    block_rows, block_cot = (
        lax.all_to_all(full_rows, "dp", split_axis=2, concat_axis=1, tiled=True),
        lax.all_to_all(full_cot, "dp", split_axis=2, concat_axis=1, tiled=True),
    )
    totals = lax.psum(live_counts, "dp").astype(jnp.float32)
    gate_part = jnp.einsum(
        "erd,edf->erf", block_rows, gate_proj, preferred_element_type=jnp.float32
    )
    up_part = jnp.einsum("erd,edf->erf", block_rows, up_proj, preferred_element_type=jnp.float32)
    cot_part = jnp.einsum("erd,efd->erf", block_cot, down_proj, preferred_element_type=jnp.float32)
    gate_total, up_total = (
        lax.psum(gate_part.astype(jnp.bfloat16), "dp").astype(jnp.float32),
        lax.psum(up_part.astype(jnp.bfloat16), "dp").astype(jnp.float32),
    )
    hidden_all = (jax.nn.silu(gate_total) * up_total).astype(jnp.bfloat16)
    cot_total = lax.psum(cot_part.astype(jnp.bfloat16), "dp").astype(jnp.float32)
    gate_all, up_all = slope_terms(gate_total, up_total, cot_total)
    scale_back = totals[:, :, None]
    grad_down_proj = (
        jnp.einsum("erf,erd->efd", hidden_all, block_cot, preferred_element_type=jnp.float32)
        / scale_back
    ).astype(jnp.bfloat16)
    grad_gate_proj = (
        jnp.einsum("erd,erf->edf", block_rows, gate_all, preferred_element_type=jnp.float32)
        / scale_back
    ).astype(jnp.bfloat16)
    grad_up_proj = (
        jnp.einsum("erd,erf->edf", block_rows, up_all, preferred_element_type=jnp.float32)
        / scale_back
    ).astype(jnp.bfloat16)
    back_term = (
        jnp.einsum("erf,edf->erd", gate_all, gate_proj, preferred_element_type=jnp.float32)
        + jnp.einsum("erf,edf->erd", up_all, up_proj, preferred_element_type=jnp.float32)
    ).astype(jnp.bfloat16)
    owned_rows = lax.all_to_all(back_term, "dp", split_axis=1, concat_axis=2, tiled=True)
    row_grads = lax.psum_scatter(
        owned_rows.astype(jnp.float32).astype(jnp.bfloat16),
        "shard",
        scatter_dimension=2,
        tiled=True,
    ).astype(jnp.float32)
    one_hot = (
        slot_tokens[:, :, None]
        == lax.broadcasted_iota(jnp.int32, (experts_here, slot_count, token_count), 2)
    ).astype(jnp.float32)
    grad_tokens = jnp.einsum("ert,erf->tf", one_hot, row_grads).astype(jnp.bfloat16)
    return (grad_tokens, grad_gate_proj, grad_up_proj, grad_down_proj)


def step_kernel(
    n_dp, n_shard,
    slot_ids, weights, live, tokens, cot, gate_hbm, up_hbm, down_hbm,
    rows_out, cotr_out, hid_out, gg_out, gu_out, tot_out, tok_out,
    gate_w, up_w, down_w, pick, full, mine, psend, precv, xsend, xrecv, back, parts, cnt, cnt_in,
    w_sem, g_send, g_recv, c_send, c_recv, b_send, b_recv, p_send, p_recv, x_send, x_recv, a_send, a_recv, r_send, r_recv,
):
    d = lax.axis_index("dp")
    s = lax.axis_index("shard")
    experts, depth, width = gate_w.shape
    feats = tokens.shape[1]
    slots = slot_ids.shape[1]
    per = n_shard // n_dp
    core = d % 2
    pair = d + 1 - 2 * core
    across = (d + 2) % 4
    half = width // 2
    piece = half // PIECES

    loads = []
    for e in range(experts):
        for i, (src, dst) in enumerate(((gate_hbm, gate_w), (up_hbm, up_w), (down_hbm, down_w))):
            load = pltpu.make_async_copy(src.at[e], dst.at[e], w_sem.at[i, e])
            load.start()
            loads.append(load)

    barrier = pltpu.get_barrier_semaphore()
    owner = s // per
    for t in range(n_shard):
        pl.semaphore_signal(barrier, inc=1, device_id={"dp": owner, "shard": t}, device_id_type=MESH)
    for e in range(n_dp):
        for k in range(per):
            pl.semaphore_signal(
                barrier, inc=1, device_id={"dp": e, "shard": d * per + k}, device_id_type=MESH
            )
    for t in range(n_shard):
        pl.semaphore_signal(barrier, inc=1, device_id={"dp": d, "shard": t}, device_id_type=MESH)
    for peer in (pair, across):
        pl.semaphore_signal(barrier, inc=1, device_id={"dp": peer, "shard": s}, device_id_type=MESH)

    count = tokens.shape[0]
    diagonal = lax.broadcasted_iota(jnp.int32, (slots, slots), 0) == lax.broadcasted_iota(
        jnp.int32, (slots, slots), 1
    )

    def as_column(row):
        wide = jnp.broadcast_to(row, (slots, slots))
        return jnp.sum(jnp.where(diagonal, wide, 0.0), axis=1, keepdims=True)

    cnt[...] = jnp.zeros_like(cnt)
    token_ids = lax.broadcasted_iota(jnp.int32, (slots, count), 1).astype(jnp.float32)
    for e in range(experts):
        alive = lax.broadcasted_iota(jnp.int32, (1, slots), 1) < live[e : e + 1, :]
        scale = as_column(weights[e : e + 1, :] * alive.astype(jnp.float32))
        chosen = as_column(slot_ids[e : e + 1, :].astype(jnp.float32)) == token_ids
        chosen = chosen.astype(jnp.float32).astype(jnp.bfloat16)
        picked = jnp.dot(chosen, tokens[...], preferred_element_type=jnp.float32)
        pick[e] = picked.astype(jnp.bfloat16)
        cots = jnp.dot(chosen, cot[...], preferred_element_type=jnp.float32)
        pick[experts + e] = (cots * scale).astype(jnp.bfloat16)
        cnt[e : e + 1, :] = jnp.broadcast_to(live[e : e + 1, :], (1, cnt.shape[1]))

    pl.semaphore_wait(barrier, 2 * n_shard + n_dp * per + 2)

    k_me = s % per
    at_me = d * per + k_me
    row_me = pl.ds(pl.multiple_of(d * slots, slots), slots)
    cuts = n_shard // (2 * experts)
    cut = feats // cuts

    def cut_cols(k, c):
        return pl.ds(pl.multiple_of(k * feats + c * cut, 128), cut)

    sends = []

    def send_to(target, is_self, pairs, send_sem_of, recv_sem_of):
        for i, (src, dst) in enumerate(pairs):
            remote = pltpu.make_async_remote_copy(
                src_ref=src, dst_ref=dst, send_sem=send_sem_of(i), recv_sem=recv_sem_of(i),
                device_id=target, device_id_type=MESH,
            )

            @pl.when(jnp.logical_not(is_self))
            def _():
                remote.start()

            @pl.when(is_self)
            def _():
                pltpu.make_async_copy(src, dst, recv_sem_of(i)).start()

            sends.append((remote, is_self))

    for step in range(n_shard):
        t = (s + step) % n_shard
        which, c = t // cuts, t % cuts
        send_to(
            {"dp": owner, "shard": t},
            jnp.logical_and(owner == d, t == s),
            (
                (pick.at[which, :, cut_cols(0, c)], full.at[which, row_me, cut_cols(k_me, c)]),
                (cnt, cnt_in.at[at_me]),
            ),
            lambda i: (g_send, c_send)[i].at[step],
            lambda i: (g_recv, c_recv)[i].at[at_me],
        )
    spread = []
    for k in range(per):
        own = full.at[s // cuts, :, cut_cols(k, s % cuts)]
        for e in range(n_dp):
            got = full.at[s // cuts, pl.ds(e * slots, slots), cut_cols(k, s % cuts)]
            pltpu.make_async_copy(got, got, g_recv.at[e * per + k]).wait()
        for step in range(1, n_shard):
            copy = pltpu.make_async_remote_copy(
                src_ref=own, dst_ref=own, send_sem=b_send.at[k, step], recv_sem=b_recv.at[k, s],
                device_id={"dp": d, "shard": (s + step) % n_shard}, device_id_type=MESH,
            )
            copy.start()
            spread.append(copy)
    for at in range(n_dp * per):
        pltpu.make_async_copy(cnt_in.at[at], cnt_in.at[at], c_recv.at[at]).wait()
    for k in range(per):
        for step in range(1, n_shard):
            t = (s + step) % n_shard
            got = full.at[t // cuts, :, cut_cols(k, t % cuts)]
            pltpu.make_async_copy(got, got, b_recv.at[k, t]).wait()
    total = cnt_in[0]
    for e in range(1, n_dp):
        total = total + cnt_in[e * per]
    tot_out[...] = 1.0 / jnp.maximum(total, 1).astype(jnp.float32)

    stages = [(e, j) for e in range(experts) for j in range(PIECES)]

    def columns(who, j):
        return pl.ds(pl.multiple_of(who * half + j * piece, 128), piece)

    def partials(e, cols):
        rows = full[e]
        gate = jnp.dot(rows, gate_w[e, :, cols], preferred_element_type=jnp.float32)
        up = jnp.dot(rows, up_w[e, :, cols], preferred_element_type=jnp.float32)
        down = lax.dot_general(
            full[experts + e], down_w[e, cols, :], (((1,), (1,)), ((), ())),
            preferred_element_type=jnp.float32,
        )
        return gate, up, down

    def pair_copy(t):
        return pltpu.make_async_remote_copy(
            src_ref=psend.at[t], dst_ref=precv.at[t], send_sem=p_send.at[t], recv_sem=p_recv.at[t],
            device_id={"dp": pair, "shard": s}, device_id_type=MESH,
        )

    def across_copy(t):
        return pltpu.make_async_remote_copy(
            src_ref=xsend.at[t], dst_ref=xrecv.at[t], send_sem=x_send.at[t], recv_sem=x_recv.at[t],
            device_id={"dp": across, "shard": s}, device_id_type=MESH,
        )

    def back_copies(t, who):
        e, j = stages[t]
        cols = columns(who, j)
        return [
            pltpu.make_async_remote_copy(
                src_ref=out.at[e, :, cols], dst_ref=out.at[e, :, cols],
                send_sem=a_send.at[i, t], recv_sem=a_recv.at[i, t],
                device_id={"dp": pair, "shard": s}, device_id_type=MESH,
            )
            for i, out in enumerate((hid_out, gg_out, gu_out))
        ]

    def compute(t):
        e, j = stages[t]
        if j == 0:
            for load in loads[3 * e : 3 * e + 3]:
                load.wait()
        for i, value in enumerate(partials(e, columns(1 - core, j))):
            psend[t, i] = value.astype(jnp.bfloat16)
        pair_copy(t).start()
        for i, value in enumerate(partials(e, columns(core, j))):
            mine[t, i] = value.astype(jnp.bfloat16)

    def add_pair(t):
        pair_copy(t).wait_recv()
        both = mine[t].astype(jnp.float32) + precv[t].astype(jnp.float32)
        xsend[t] = both.astype(jnp.bfloat16)
        across_copy(t).start()

    def finish(t):
        e, j = stages[t]
        across_copy(t).wait_recv()
        gate = xsend[t, 0].astype(jnp.float32) + xrecv[t, 0].astype(jnp.float32)
        up = xsend[t, 1].astype(jnp.float32) + xrecv[t, 1].astype(jnp.float32)
        cot_hidden = xsend[t, 2].astype(jnp.float32) + xrecv[t, 2].astype(jnp.float32)
        cols = columns(core, j)
        hid_out[e, :, cols] = (jax.nn.silu(gate) * up).astype(jnp.bfloat16)
        grad_gate, grad_up = slope_terms(gate, up, cot_hidden)
        gg_out[e, :, cols] = grad_gate
        gu_out[e, :, cols] = grad_up
        for copy in back_copies(t, core):
            copy.start()

    def backward(e):
        for t, (te, _) in enumerate(stages):
            if te == e:
                for copy in back_copies(t, 1 - core):
                    copy.wait_recv()
        contract = (((1,), (1,)), ((), ()))
        block = 256 if depth % 256 == 0 else depth
        for b in range(depth // block):
            r = pl.ds(b * block, block)
            term = lax.dot_general(
                gg_out[e], gate_w[e, r, :], contract, preferred_element_type=jnp.float32
            ) + lax.dot_general(
                gu_out[e], up_w[e, r, :], contract, preferred_element_type=jnp.float32
            )
            back[e, :, r] = term.astype(jnp.bfloat16)
        for step in range(n_dp):
            who = (d + step) % n_dp
            r = pl.ds(pl.multiple_of(who * slots, slots), slots)
            for k in range(per):
                send_to(
                    {"dp": who, "shard": d * per + k},
                    jnp.logical_and(who == d, d * per + k == s),
                    ((back.at[e, r, pl.ds(k * feats, feats)], parts.at[e, s]),),
                    lambda i: r_send.at[e, step * per + k],
                    lambda i: r_recv.at[e, s],
                )

    last = len(stages)
    for t in range(last):
        compute(t)
        if t >= 1:
            add_pair(t - 1)
        if t >= 2:
            finish(t - 2)
    add_pair(last - 1)
    for e in range(experts):
        rows_out[e] = full[e]
        cotr_out[e] = full[experts + e]
    finish(last - 2)
    for e in range(experts - 1):
        backward(e)
    finish(last - 1)
    backward(experts - 1)

    result = jnp.zeros(tokens.shape, jnp.float32)
    places = lax.broadcasted_iota(jnp.int32, (count, slots), 0)
    for e in range(experts):
        for t in range(n_shard):
            pltpu.make_async_copy(parts.at[e, t], parts.at[e, t], r_recv.at[e, t]).wait()
        acc = parts[e, 0].astype(jnp.float32)
        for t in range(1, n_shard):
            acc = acc + parts[e, t].astype(jnp.float32)
        chosen = (slot_ids[e : e + 1, :] == places).astype(jnp.float32)
        result = result + jnp.dot(
            chosen, acc, preferred_element_type=jnp.float32, precision=lax.Precision.HIGHEST
        )
    tok_out[...] = result.astype(jnp.bfloat16)

    for copy in spread:
        copy.wait_send()
    for t in range(last):
        pair_copy(t).wait_send()
        across_copy(t).wait_send()
        for copy in back_copies(t, core):
            copy.wait_send()
    for remote, is_self in sends:

        @pl.when(jnp.logical_not(is_self))
        def _():
            remote.wait_send()


def outer_kernel(rows, cots, hidden, gate, up, scale, gate_out, up_out, down_out):
    e = pl.program_id(0)
    factor = scale[pl.ds(e, 1), :][:, :1]

    def fill(left, right, out):
        wide = right.shape[2]
        step = 256 if wide % 256 == 0 else wide
        for b in range(wide // step):
            c = pl.ds(b * step, step)
            value = lax.dot_general(
                left[0], right[0, :, c], (((0,), (0,)), ((), ())),
                preferred_element_type=jnp.float32,
            )
            out[0, :, c] = (value * factor).astype(jnp.bfloat16)

    fill(rows, gate, gate_out)
    fill(rows, up, up_out)
    fill(hidden, cots, down_out)


def weight_grads(rows, cots, hidden, gate, up, scale):
    experts, routed, depth = rows.shape
    width = hidden.shape[2]
    blocks = 4
    tall, long = depth // blocks, width // blocks
    bf16 = jnp.bfloat16
    whole = lambda n: pl.BlockSpec((1, routed, n), lambda e, b: (e, 0, 0))
    part = lambda n: pl.BlockSpec((1, routed, n), lambda e, b: (e, 0, b))
    wide_out = pl.BlockSpec((1, tall, width), lambda e, b: (e, b, 0))
    down_out = pl.BlockSpec((1, long, depth), lambda e, b: (e, b, 0))
    return pl.pallas_call(
        outer_kernel,
        grid=(experts, blocks),
        out_shape=(
            jax.ShapeDtypeStruct((experts, depth, width), bf16),
            jax.ShapeDtypeStruct((experts, depth, width), bf16),
            jax.ShapeDtypeStruct((experts, width, depth), bf16),
        ),
        in_specs=[
            part(tall), whole(depth), part(long), whole(width), whole(width),
            pl.BlockSpec(scale.shape, lambda e, b: (0, 0)),
        ],
        out_specs=(wide_out, wide_out, down_out),
        compiler_params=pltpu.CompilerParams(vmem_limit_bytes=62 * 1024 * 1024),
        name="weight_grads",
    )(rows, cots, hidden, gate, up, scale)


def on_device_fused(
    n_dp, n_shard,
    tokens, cotangent, gate_proj, up_proj, down_proj, slot_tokens, gate_weights, live_counts,
):
    experts, slots = slot_tokens.shape
    depth, width = gate_proj.shape[1:]
    feats = tokens.shape[1]
    routed = slots * n_dp
    per = n_shard // n_dp
    stages = experts * PIECES
    piece = width // 2 // PIECES
    vmem = pl.BlockSpec(memory_space=pltpu.VMEM)
    hbm = pl.BlockSpec(memory_space=pl.ANY)
    bf16 = jnp.bfloat16
    dma = pltpu.SemaphoreType.DMA
    block = pltpu.VMEM((stages, 3, routed, piece), bf16)
    outs = pl.pallas_call(
        functools.partial(step_kernel, n_dp, n_shard),
        out_shape=(
            jax.ShapeDtypeStruct((experts, routed, depth), bf16),
            jax.ShapeDtypeStruct((experts, routed, depth), bf16),
            jax.ShapeDtypeStruct((experts, routed, width), bf16),
            jax.ShapeDtypeStruct((experts, routed, width), bf16),
            jax.ShapeDtypeStruct((experts, routed, width), bf16),
            jax.ShapeDtypeStruct((8, 128), jnp.float32),
            jax.ShapeDtypeStruct(tokens.shape, bf16),
        ),
        in_specs=[vmem] * 5 + [hbm] * 3,
        out_specs=(vmem,) * 7,
        scratch_shapes=[
            pltpu.VMEM((experts, depth, width), bf16),
            pltpu.VMEM((experts, depth, width), bf16),
            pltpu.VMEM((experts, width, depth), bf16),
            pltpu.VMEM((2 * experts, slots, feats), bf16),
            pltpu.VMEM((2 * experts, routed, depth), bf16),
            block, block, block, block, block,
            pltpu.VMEM((experts, routed, depth), bf16),
            pltpu.VMEM((experts, n_shard, slots, feats), bf16),
            pltpu.VMEM((8, 128), jnp.int32),
            pltpu.VMEM((n_dp * per, 8, 128), jnp.int32),
            dma((3, experts)),
            dma((n_shard,)), dma((n_dp * per,)), dma((n_shard,)), dma((n_dp * per,)),
            dma((per, n_shard)), dma((per, n_shard)),
            dma((stages,)), dma((stages,)), dma((stages,)), dma((stages,)),
            dma((3, stages)), dma((3, stages)),
            dma((experts, n_dp * per)), dma((experts, n_shard)),
        ],
        compiler_params=pltpu.CompilerParams(
            collective_id=0, has_side_effects=True, vmem_limit_bytes=62 * 1024 * 1024
        ),
        name="route_step",
    )(
        slot_tokens, gate_weights, live_counts, tokens, cotangent, gate_proj, up_proj, down_proj,
    )
    block_rows, block_cot, hidden_all, gate_all, up_all, scale, grad_tokens = outs
    grads = weight_grads(block_rows, block_cot, hidden_all, gate_all, up_all, scale)
    return (grad_tokens, *grads)


def pick_form(n_dp, n_shard, *args):
    feats, experts = args[0].shape[1], args[2].shape[0]
    depth, width = args[2].shape[1:]
    cuts = n_shard // (2 * experts)
    even = n_dp == 4 and n_shard % n_dp == 0 and n_shard == 2 * experts * cuts
    aligned = even and experts <= 8 and feats % (128 * cuts) == 0 and depth % 512 == 0
    if aligned and width % (256 * PIECES) == 0 and width % 512 == 0 and args[5].shape[1] % 16 == 0:
        return on_device_fused(n_dp, n_shard, *args)
    return on_device(*args)


def solution(mesh):
    in_specs = (
        P("dp", "shard"),
        P("dp", "shard"),
        P(None, "dp", "shard"),
        P(None, "dp", "shard"),
        P(None, "shard", "dp"),
        P(None, "dp"),
        P(None, "dp"),
        P(None, "dp"),
    )
    out_specs = (
        P("dp", "shard"),
        P(None, "dp", "shard"),
        P(None, "dp", "shard"),
        P(None, "shard", "dp"),
    )
    return jax.shard_map(
        functools.partial(pick_form, mesh.shape["dp"], mesh.shape["shard"]), mesh=mesh, in_specs=in_specs, out_specs=out_specs, check_vma=False
    )
```

```python
import functools

import jax
import jax.numpy as jnp
from jax import lax
from jax.experimental import pallas as pl
from jax.experimental.pallas import tpu as pltpu
from jax.sharding import PartitionSpec as P

MESH = pl.DeviceIdType.MESH
PIECES = 2


def slope_terms(gate_sum, up_sum, cot_hidden):
    sigmoid_part = jax.nn.sigmoid(gate_sum)
    grad_gate = (
        cot_hidden * up_sum * sigmoid_part * (1.0 + gate_sum * (1.0 - sigmoid_part))
    ).astype(jnp.bfloat16)
    grad_up = (cot_hidden * gate_sum * sigmoid_part).astype(jnp.bfloat16)
    return (grad_gate, grad_up)


def on_device(
    tokens, cotangent, gate_proj, up_proj, down_proj, slot_tokens, gate_weights, live_counts
):
    experts_here = slot_tokens.shape[0]
    slot_count = slot_tokens.shape[1]
    token_count = tokens.shape[0]
    position = lax.broadcasted_iota(jnp.int32, slot_tokens.shape, 1)
    alive_mask = (position < live_counts).astype(jnp.float32)
    picked = tokens[slot_tokens]
    weighted = (
        cotangent[slot_tokens].astype(jnp.float32) * (gate_weights * alive_mask)[:, :, None]
    ).astype(jnp.bfloat16)
    full_rows, full_cot = (
        lax.all_gather(picked, "shard", axis=2, tiled=True),
        lax.all_gather(weighted, "shard", axis=2, tiled=True),
    )
    block_rows, block_cot = (
        lax.all_to_all(full_rows, "dp", split_axis=2, concat_axis=1, tiled=True),
        lax.all_to_all(full_cot, "dp", split_axis=2, concat_axis=1, tiled=True),
    )
    totals = lax.psum(live_counts, "dp").astype(jnp.float32)
    gate_part = jnp.einsum(
        "erd,edf->erf", block_rows, gate_proj, preferred_element_type=jnp.float32
    )
    up_part = jnp.einsum("erd,edf->erf", block_rows, up_proj, preferred_element_type=jnp.float32)
    cot_part = jnp.einsum("erd,efd->erf", block_cot, down_proj, preferred_element_type=jnp.float32)
    gate_total, up_total = (
        lax.psum(gate_part.astype(jnp.bfloat16), "dp").astype(jnp.float32),
        lax.psum(up_part.astype(jnp.bfloat16), "dp").astype(jnp.float32),
    )
    hidden_all = (jax.nn.silu(gate_total) * up_total).astype(jnp.bfloat16)
    cot_total = lax.psum(cot_part.astype(jnp.bfloat16), "dp").astype(jnp.float32)
    gate_all, up_all = slope_terms(gate_total, up_total, cot_total)
    scale_back = totals[:, :, None]
    grad_down_proj = (
        jnp.einsum("erf,erd->efd", hidden_all, block_cot, preferred_element_type=jnp.float32)
        / scale_back
    ).astype(jnp.bfloat16)
    grad_gate_proj = (
        jnp.einsum("erd,erf->edf", block_rows, gate_all, preferred_element_type=jnp.float32)
        / scale_back
    ).astype(jnp.bfloat16)
    grad_up_proj = (
        jnp.einsum("erd,erf->edf", block_rows, up_all, preferred_element_type=jnp.float32)
        / scale_back
    ).astype(jnp.bfloat16)
    back_term = (
        jnp.einsum("erf,edf->erd", gate_all, gate_proj, preferred_element_type=jnp.float32)
        + jnp.einsum("erf,edf->erd", up_all, up_proj, preferred_element_type=jnp.float32)
    ).astype(jnp.bfloat16)
    owned_rows = lax.all_to_all(back_term, "dp", split_axis=1, concat_axis=2, tiled=True)
    row_grads = lax.psum_scatter(
        owned_rows.astype(jnp.float32).astype(jnp.bfloat16),
        "shard",
        scatter_dimension=2,
        tiled=True,
    ).astype(jnp.float32)
    one_hot = (
        slot_tokens[:, :, None]
        == lax.broadcasted_iota(jnp.int32, (experts_here, slot_count, token_count), 2)
    ).astype(jnp.float32)
    grad_tokens = jnp.einsum("ert,erf->tf", one_hot, row_grads).astype(jnp.bfloat16)
    return (grad_tokens, grad_gate_proj, grad_up_proj, grad_down_proj)


def step_kernel(
    n_dp, n_shard,
    slot_ids, weights, live, tokens, cot, gate_hbm, up_hbm, down_hbm,
    rows_out, cotr_out, hid_out, gg_out, gu_out, tot_out, tok_out,
    gate_w, up_w, down_w, pick, full, mine, psend, precv, xsend, xrecv, back, parts, cnt, cnt_in,
    w_sem, g_send, g_recv, c_send, c_recv, b_send, b_recv, p_send, p_recv, x_send, x_recv, a_send, a_recv, r_send, r_recv,
):
    d = lax.axis_index("dp")
    s = lax.axis_index("shard")
    experts, depth, width = gate_w.shape
    feats = tokens.shape[1]
    slots = slot_ids.shape[1]
    per = n_shard // n_dp
    core = d % 2
    pair = d + 1 - 2 * core
    across = (d + 2) % 4
    half = width // 2
    piece = half // PIECES

    loads = []
    for e in range(experts):
        for i, (src, dst) in enumerate(((gate_hbm, gate_w), (up_hbm, up_w), (down_hbm, down_w))):
            load = pltpu.make_async_copy(src.at[e], dst.at[e], w_sem.at[i, e])
            load.start()
            loads.append(load)

    barrier = pltpu.get_barrier_semaphore()
    owner = s // per
    for t in range(n_shard):
        pl.semaphore_signal(barrier, inc=1, device_id={"dp": owner, "shard": t}, device_id_type=MESH)
    for e in range(n_dp):
        for k in range(per):
            pl.semaphore_signal(
                barrier, inc=1, device_id={"dp": e, "shard": d * per + k}, device_id_type=MESH
            )
    for t in range(n_shard):
        pl.semaphore_signal(barrier, inc=1, device_id={"dp": d, "shard": t}, device_id_type=MESH)
    for peer in (pair, across):
        pl.semaphore_signal(barrier, inc=1, device_id={"dp": peer, "shard": s}, device_id_type=MESH)

    count = tokens.shape[0]
    diagonal = lax.broadcasted_iota(jnp.int32, (slots, slots), 0) == lax.broadcasted_iota(
        jnp.int32, (slots, slots), 1
    )

    def as_column(row):
        wide = jnp.broadcast_to(row, (slots, slots))
        return jnp.sum(jnp.where(diagonal, wide, 0.0), axis=1, keepdims=True)

    cnt[...] = jnp.zeros_like(cnt)
    token_ids = lax.broadcasted_iota(jnp.int32, (slots, count), 1).astype(jnp.float32)
    for e in range(experts):
        alive = lax.broadcasted_iota(jnp.int32, (1, slots), 1) < live[e : e + 1, :]
        scale = as_column(weights[e : e + 1, :] * alive.astype(jnp.float32))
        chosen = as_column(slot_ids[e : e + 1, :].astype(jnp.float32)) == token_ids
        chosen = chosen.astype(jnp.float32).astype(jnp.bfloat16)
        picked = jnp.dot(chosen, tokens[...], preferred_element_type=jnp.float32)
        pick[e] = picked.astype(jnp.bfloat16)
        cots = jnp.dot(chosen, cot[...], preferred_element_type=jnp.float32)
        pick[experts + e] = (cots * scale).astype(jnp.bfloat16)
        cnt[e : e + 1, :] = jnp.broadcast_to(live[e : e + 1, :], (1, cnt.shape[1]))

    pl.semaphore_wait(barrier, 2 * n_shard + n_dp * per + 2)

    k_me = s % per
    at_me = d * per + k_me
    row_me = pl.ds(pl.multiple_of(d * slots, slots), slots)
    cuts = n_shard // (2 * experts)
    cut = feats // cuts

    def cut_cols(k, c):
        return pl.ds(pl.multiple_of(k * feats + c * cut, 128), cut)

    sends = []

    def send_to(target, is_self, pairs, send_sem_of, recv_sem_of):
        for i, (src, dst) in enumerate(pairs):
            remote = pltpu.make_async_remote_copy(
                src_ref=src, dst_ref=dst, send_sem=send_sem_of(i), recv_sem=recv_sem_of(i),
                device_id=target, device_id_type=MESH,
            )

            @pl.when(jnp.logical_not(is_self))
            def _():
                remote.start()

            @pl.when(is_self)
            def _():
                pltpu.make_async_copy(src, dst, recv_sem_of(i)).start()

            sends.append((remote, is_self))

    for step in range(n_shard):
        t = (s + step) % n_shard
        which, c = t // cuts, t % cuts
        send_to(
            {"dp": owner, "shard": t},
            jnp.logical_and(owner == d, t == s),
            (
                (pick.at[which, :, cut_cols(0, c)], full.at[which, row_me, cut_cols(k_me, c)]),
                (cnt, cnt_in.at[at_me]),
            ),
            lambda i: (g_send, c_send)[i].at[step],
            lambda i: (g_recv, c_recv)[i].at[at_me],
        )
    spread = []
    side = s + 1 - 2 * (s % 2)

    def share(ref, k, source, lane, target):
        copy = pltpu.make_async_remote_copy(
            src_ref=ref, dst_ref=ref, send_sem=b_send.at[k, lane], recv_sem=b_recv.at[k, source],
            device_id={"dp": d, "shard": target}, device_id_type=MESH,
        )
        copy.start()
        spread.append(copy)

    def arrived(k, t):
        got = full.at[t // cuts, :, cut_cols(k, t % cuts)]
        pltpu.make_async_copy(got, got, b_recv.at[k, t]).wait()
        return got

    for k in range(per):
        own = full.at[s // cuts, :, cut_cols(k, s % cuts)]
        for e in range(n_dp):
            got = full.at[s // cuts, pl.ds(e * slots, slots), cut_cols(k, s % cuts)]
            pltpu.make_async_copy(got, got, g_recv.at[e * per + k]).wait()
        share(own, k, s, 0, side)
        for step in range(1, n_shard // 2):
            share(own, k, s, step, (s + 2 * step) % n_shard)
    for at in range(n_dp * per):
        pltpu.make_async_copy(cnt_in.at[at], cnt_in.at[at], c_recv.at[at]).wait()
    for step in range(1, n_shard // 2):
        t = (s + 2 * step) % n_shard
        for k in range(per):
            share(arrived(k, t), k, t, n_shard // 2 + step, side)
    for step in range(n_shard // 2):
        for k in range(per):
            arrived(k, (side + 2 * step) % n_shard)
    total = cnt_in[0]
    for e in range(1, n_dp):
        total = total + cnt_in[e * per]
    tot_out[...] = 1.0 / jnp.maximum(total, 1).astype(jnp.float32)

    stages = [(e, j) for e in range(experts) for j in range(PIECES)]

    def columns(who, j):
        return pl.ds(pl.multiple_of(who * half + j * piece, 128), piece)

    def partials(e, cols):
        rows = full[e]
        gate = jnp.dot(rows, gate_w[e, :, cols], preferred_element_type=jnp.float32)
        up = jnp.dot(rows, up_w[e, :, cols], preferred_element_type=jnp.float32)
        down = lax.dot_general(
            full[experts + e], down_w[e, cols, :], (((1,), (1,)), ((), ())),
            preferred_element_type=jnp.float32,
        )
        return gate, up, down

    def pair_copy(t):
        return pltpu.make_async_remote_copy(
            src_ref=psend.at[t], dst_ref=precv.at[t], send_sem=p_send.at[t], recv_sem=p_recv.at[t],
            device_id={"dp": pair, "shard": s}, device_id_type=MESH,
        )

    def across_copy(t):
        return pltpu.make_async_remote_copy(
            src_ref=xsend.at[t], dst_ref=xrecv.at[t], send_sem=x_send.at[t], recv_sem=x_recv.at[t],
            device_id={"dp": across, "shard": s}, device_id_type=MESH,
        )

    def back_copies(t, who):
        e, j = stages[t]
        cols = columns(who, j)
        return [
            pltpu.make_async_remote_copy(
                src_ref=out.at[e, :, cols], dst_ref=out.at[e, :, cols],
                send_sem=a_send.at[i, t], recv_sem=a_recv.at[i, t],
                device_id={"dp": pair, "shard": s}, device_id_type=MESH,
            )
            for i, out in enumerate((hid_out, gg_out, gu_out))
        ]

    def compute(t):
        e, j = stages[t]
        if j == 0:
            for load in loads[3 * e : 3 * e + 3]:
                load.wait()
        for i, value in enumerate(partials(e, columns(1 - core, j))):
            psend[t, i] = value.astype(jnp.bfloat16)
        pair_copy(t).start()
        for i, value in enumerate(partials(e, columns(core, j))):
            mine[t, i] = value.astype(jnp.bfloat16)

    def add_pair(t):
        pair_copy(t).wait_recv()
        both = mine[t].astype(jnp.float32) + precv[t].astype(jnp.float32)
        xsend[t] = both.astype(jnp.bfloat16)
        across_copy(t).start()

    def finish(t):
        e, j = stages[t]
        across_copy(t).wait_recv()
        gate = xsend[t, 0].astype(jnp.float32) + xrecv[t, 0].astype(jnp.float32)
        up = xsend[t, 1].astype(jnp.float32) + xrecv[t, 1].astype(jnp.float32)
        cot_hidden = xsend[t, 2].astype(jnp.float32) + xrecv[t, 2].astype(jnp.float32)
        cols = columns(core, j)
        hid_out[e, :, cols] = (jax.nn.silu(gate) * up).astype(jnp.bfloat16)
        grad_gate, grad_up = slope_terms(gate, up, cot_hidden)
        gg_out[e, :, cols] = grad_gate
        gu_out[e, :, cols] = grad_up
        for copy in back_copies(t, core):
            copy.start()

    def backward(e):
        for t, (te, _) in enumerate(stages):
            if te == e:
                for copy in back_copies(t, 1 - core):
                    copy.wait_recv()
        contract = (((1,), (1,)), ((), ()))
        block = 256 if depth % 256 == 0 else depth
        for b in range(depth // block):
            r = pl.ds(b * block, block)
            term = lax.dot_general(
                gg_out[e], gate_w[e, r, :], contract, preferred_element_type=jnp.float32
            ) + lax.dot_general(
                gu_out[e], up_w[e, r, :], contract, preferred_element_type=jnp.float32
            )
            back[e, :, r] = term.astype(jnp.bfloat16)
        for step in range(n_dp):
            who = (d + step) % n_dp
            r = pl.ds(pl.multiple_of(who * slots, slots), slots)
            for k in range(per):
                send_to(
                    {"dp": who, "shard": d * per + k},
                    jnp.logical_and(who == d, d * per + k == s),
                    ((back.at[e, r, pl.ds(k * feats, feats)], parts.at[e, s]),),
                    lambda i: r_send.at[e, step * per + k],
                    lambda i: r_recv.at[e, s],
                )

    last = len(stages)
    for t in range(last):
        compute(t)
        if t >= 1:
            add_pair(t - 1)
        if t >= 2:
            finish(t - 2)
    add_pair(last - 1)
    for e in range(experts):
        rows_out[e] = full[e]
        cotr_out[e] = full[experts + e]
    finish(last - 2)
    for e in range(experts - 1):
        backward(e)
    finish(last - 1)
    backward(experts - 1)

    result = jnp.zeros(tokens.shape, jnp.float32)
    places = lax.broadcasted_iota(jnp.int32, (count, slots), 0)
    for e in range(experts):
        for t in range(n_shard):
            pltpu.make_async_copy(parts.at[e, t], parts.at[e, t], r_recv.at[e, t]).wait()
        acc = parts[e, 0].astype(jnp.float32)
        for t in range(1, n_shard):
            acc = acc + parts[e, t].astype(jnp.float32)
        chosen = (slot_ids[e : e + 1, :] == places).astype(jnp.float32)
        result = result + jnp.dot(
            chosen, acc, preferred_element_type=jnp.float32, precision=lax.Precision.HIGHEST
        )
    tok_out[...] = result.astype(jnp.bfloat16)

    for copy in spread:
        copy.wait_send()
    for t in range(last):
        pair_copy(t).wait_send()
        across_copy(t).wait_send()
        for copy in back_copies(t, core):
            copy.wait_send()
    for remote, is_self in sends:

        @pl.when(jnp.logical_not(is_self))
        def _():
            remote.wait_send()


def outer_kernel(rows, cots, hidden, gate, up, scale, gate_out, up_out, down_out):
    e = pl.program_id(0)
    factor = scale[pl.ds(e, 1), :][:, :1]

    def fill(left, right, out):
        wide = right.shape[2]
        step = 256 if wide % 256 == 0 else wide
        for b in range(wide // step):
            c = pl.ds(b * step, step)
            value = lax.dot_general(
                left[0], right[0, :, c], (((0,), (0,)), ((), ())),
                preferred_element_type=jnp.float32,
            )
            out[0, :, c] = (value * factor).astype(jnp.bfloat16)

    fill(rows, gate, gate_out)
    fill(rows, up, up_out)
    fill(hidden, cots, down_out)


def weight_grads(rows, cots, hidden, gate, up, scale):
    experts, routed, depth = rows.shape
    width = hidden.shape[2]
    blocks = 4
    tall, long = depth // blocks, width // blocks
    bf16 = jnp.bfloat16
    whole = lambda n: pl.BlockSpec((1, routed, n), lambda e, b: (e, 0, 0))
    part = lambda n: pl.BlockSpec((1, routed, n), lambda e, b: (e, 0, b))
    wide_out = pl.BlockSpec((1, tall, width), lambda e, b: (e, b, 0))
    down_out = pl.BlockSpec((1, long, depth), lambda e, b: (e, b, 0))
    return pl.pallas_call(
        outer_kernel,
        grid=(experts, blocks),
        out_shape=(
            jax.ShapeDtypeStruct((experts, depth, width), bf16),
            jax.ShapeDtypeStruct((experts, depth, width), bf16),
            jax.ShapeDtypeStruct((experts, width, depth), bf16),
        ),
        in_specs=[
            part(tall), whole(depth), part(long), whole(width), whole(width),
            pl.BlockSpec(scale.shape, lambda e, b: (0, 0)),
        ],
        out_specs=(wide_out, wide_out, down_out),
        compiler_params=pltpu.CompilerParams(vmem_limit_bytes=62 * 1024 * 1024),
        name="weight_grads",
    )(rows, cots, hidden, gate, up, scale)


def on_device_fused(
    n_dp, n_shard,
    tokens, cotangent, gate_proj, up_proj, down_proj, slot_tokens, gate_weights, live_counts,
):
    experts, slots = slot_tokens.shape
    depth, width = gate_proj.shape[1:]
    feats = tokens.shape[1]
    routed = slots * n_dp
    per = n_shard // n_dp
    stages = experts * PIECES
    piece = width // 2 // PIECES
    vmem = pl.BlockSpec(memory_space=pltpu.VMEM)
    hbm = pl.BlockSpec(memory_space=pl.ANY)
    bf16 = jnp.bfloat16
    dma = pltpu.SemaphoreType.DMA
    block = pltpu.VMEM((stages, 3, routed, piece), bf16)
    outs = pl.pallas_call(
        functools.partial(step_kernel, n_dp, n_shard),
        out_shape=(
            jax.ShapeDtypeStruct((experts, routed, depth), bf16),
            jax.ShapeDtypeStruct((experts, routed, depth), bf16),
            jax.ShapeDtypeStruct((experts, routed, width), bf16),
            jax.ShapeDtypeStruct((experts, routed, width), bf16),
            jax.ShapeDtypeStruct((experts, routed, width), bf16),
            jax.ShapeDtypeStruct((8, 128), jnp.float32),
            jax.ShapeDtypeStruct(tokens.shape, bf16),
        ),
        in_specs=[vmem] * 5 + [hbm] * 3,
        out_specs=(vmem,) * 7,
        scratch_shapes=[
            pltpu.VMEM((experts, depth, width), bf16),
            pltpu.VMEM((experts, depth, width), bf16),
            pltpu.VMEM((experts, width, depth), bf16),
            pltpu.VMEM((2 * experts, slots, feats), bf16),
            pltpu.VMEM((2 * experts, routed, depth), bf16),
            block, block, block, block, block,
            pltpu.VMEM((experts, routed, depth), bf16),
            pltpu.VMEM((experts, n_shard, slots, feats), bf16),
            pltpu.VMEM((8, 128), jnp.int32),
            pltpu.VMEM((n_dp * per, 8, 128), jnp.int32),
            dma((3, experts)),
            dma((n_shard,)), dma((n_dp * per,)), dma((n_shard,)), dma((n_dp * per,)),
            dma((per, n_shard)), dma((per, n_shard)),
            dma((stages,)), dma((stages,)), dma((stages,)), dma((stages,)),
            dma((3, stages)), dma((3, stages)),
            dma((experts, n_dp * per)), dma((experts, n_shard)),
        ],
        compiler_params=pltpu.CompilerParams(
            collective_id=0, has_side_effects=True, vmem_limit_bytes=62 * 1024 * 1024
        ),
        name="route_step",
    )(
        slot_tokens, gate_weights, live_counts, tokens, cotangent, gate_proj, up_proj, down_proj,
    )
    block_rows, block_cot, hidden_all, gate_all, up_all, scale, grad_tokens = outs
    grads = weight_grads(block_rows, block_cot, hidden_all, gate_all, up_all, scale)
    return (grad_tokens, *grads)


def pick_form(n_dp, n_shard, *args):
    feats, experts = args[0].shape[1], args[2].shape[0]
    depth, width = args[2].shape[1:]
    cuts = n_shard // (2 * experts)
    even = n_dp == 4 and n_shard % n_dp == 0 and n_shard == 2 * experts * cuts
    aligned = even and experts <= 8 and feats % (128 * cuts) == 0 and depth % 512 == 0
    if aligned and width % (256 * PIECES) == 0 and width % 512 == 0 and args[5].shape[1] % 16 == 0:
        return on_device_fused(n_dp, n_shard, *args)
    return on_device(*args)


def solution(mesh):
    in_specs = (
        P("dp", "shard"),
        P("dp", "shard"),
        P(None, "dp", "shard"),
        P(None, "dp", "shard"),
        P(None, "shard", "dp"),
        P(None, "dp"),
        P(None, "dp"),
        P(None, "dp"),
    )
    out_specs = (
        P("dp", "shard"),
        P(None, "dp", "shard"),
        P(None, "dp", "shard"),
        P(None, "shard", "dp"),
    )
    return jax.shard_map(
        functools.partial(pick_form, mesh.shape["dp"], mesh.shape["shard"]), mesh=mesh, in_specs=in_specs, out_specs=out_specs, check_vma=False
    )
```
